32 devices in a mesh: fact: 4 (over z), dim: 8 (over y, x, core).
Axes of the slice: x: 2, y: 2, z: 4, core: 2. Of those that a mesh axis runs over, the one named last changes fastest.
Arguments:
- facts: bfloat16 [4096, 512], P(('fact', 'dim')), may hold values from -6 to 6
- dims: bfloat16 [4096, 512], P(('fact', 'dim')), may hold values from -6 to 6
- tiles: bfloat16 [1024, 128, 128], P(('fact', 'dim')), may hold values from -0.125 to 0.125
- links: int32 [1024, 2], P(('fact', 'dim')), may hold values from 0 to 31, as said below
- link_count: int32 [32], P(('fact', 'dim')), may hold values from 8 to 32, as said below
- block_table: int32 [32], replicated, may hold values from 0 to 2
- w_self: bfloat16 [512, 512], replicated, may hold values from -0.25 to 0.25
- w_tables: bfloat16 [3, 512, 512], replicated, may hold values from -0.25 to 0.25
- cot: bfloat16 [4096, 512], P(('fact', 'dim')), may hold values from -6 to 6
Outputs:
- fact_out: bfloat16 [4096, 512], P(('fact', 'dim'))
- grad_dims: float32 [4096, 512], P(('fact', 'dim'))
- grad_w_self: float32 [512, 512], replicated
- grad_w_tables: float32 [3, 512, 512], replicated
The draws below stay inside these ranges and needn't reach their ends.
Inputs may be any that keep to these rules, and one draw needn't show every extreme that they name: On device k = f * 8 + d (f, d its fact and dim indices), links[l,0] is a fact block among those of rows f * 128 * 8 to (f + 1) * 128 * 8 - 1, and links[l,1] is a dimension block held by a device with dim index d, i.e. links[l,1] % 8 == d. Slots beyond the device's count hold such indices too and are padding. `link_count`: some device has all 32 slots live and some device exactly 8.
All inputs are finite; a program needn't handle non-finite values.
Results may differ from the reference program's by a relative error of at most 0.017.
Values may be sent and summed in bfloat16 or wider, within the bound.
A program may use at most 64 MiB of HBM per device.

```python
import jax
import jax.numpy as jnp
from jax import lax

D = 512
TABLES = 3
BLOCK = 128
FACT_DEV = 128
DIM_DEV = 128
LINKS_DEV = 32
NF = 4096
ND = 4096
LINKS = 1024
DBLOCKS = 32
N_FACT = 4
N_DIM = 8


def draw_links(key, part):
    devices = N_FACT * N_DIM
    first, second, third = jax.random.split(key, 3)
    device = jnp.arange(devices, dtype=jnp.int32)
    fact_index = device // N_DIM
    dim_index = device % N_DIM
    fact_blocks = FACT_DEV * N_DIM // BLOCK
    per_owner = DIM_DEV // BLOCK
    fact_off = jax.random.randint(first, (devices, LINKS_DEV), 0, fact_blocks)
    holder = jax.random.randint(second, (devices, LINKS_DEV), 0, N_FACT)
    within = jax.random.randint(third, (devices, LINKS_DEV), 0, per_owner)
    slot = jnp.arange(LINKS_DEV, dtype=jnp.int32)
    first_dev = (device[:, None] == 0) & (slot[None, :] == 0)
    last_dev = (device[:, None] == devices - 1) & (slot[None, :] == 0)
    fact_off = jnp.where(first_dev, 0, jnp.where(last_dev, fact_blocks - 1, fact_off))
    holder = jnp.where(first_dev, 0, jnp.where(last_dev, N_FACT - 1, holder))
    within = jnp.where(first_dev, 0, jnp.where(last_dev, per_owner - 1, within))
    fact_blk = fact_index[:, None] * fact_blocks + fact_off
    dim_blk = (holder * N_DIM + dim_index[:, None]) * per_owner + within
    return jnp.stack([fact_blk, dim_blk], axis=-1).reshape(devices * LINKS_DEV, 2).astype(jnp.int32)


def draw_link_count(key, part):
    devices = N_FACT * N_DIM
    first, second, third = jax.random.split(key, 3)
    lowest = LINKS_DEV // 4
    counts = jax.random.randint(first, (devices,), lowest, LINKS_DEV + 1)
    busiest = jax.random.randint(second, (), 0, devices)
    lightest = (busiest + 1 + jax.random.randint(third, (), 0, devices - 1)) % devices
    device = jnp.arange(devices, dtype=jnp.int32)
    counts = jnp.where(device == busiest, LINKS_DEV, counts)
    counts = jnp.where(device == lightest, lowest, counts)
    return counts.astype(jnp.int32)


def place_ends(values, key, least, largest):
    shape = values.shape
    index_at = [jax.random.randint(jax.random.fold_in(key, axis), (), 0, shape[axis]) for axis in range(len(shape))]
    values = values.at[tuple(index_at)].set(least)
    longest = shape.index(max(shape))
    index_at[longest] = (index_at[longest] + 1) % shape[longest]
    return values.at[tuple(index_at)].set(largest)


def level_of(rng, shape, cuts, low, top_value):
    loudness, own = 1.0, jax.random.fold_in(rng, 6)
    for position, blocks in cuts:
        heights = jnp.exp(jax.random.uniform(jax.random.fold_in(own, position), (blocks,), jnp.float32, low / len(cuts), top_value / len(cuts)))
        loudness = loudness * jnp.repeat(heights, shape[position] // blocks).reshape([-1 if axis == position else 1 for axis in range(len(shape))])
    return loudness


def centred(rng, shape, spread, most, cuts=(), held_as=jnp.bfloat16):
    loudness = level_of(rng, shape, cuts, -0.22, 0.18) if cuts else 1.0
    entries = jax.random.normal(rng, shape, jnp.float32) * spread * loudness
    return jnp.minimum(jnp.maximum(entries, -most), most).astype(held_as)


def setup_inputs(seed: int = 0) -> dict:
    streams_of = jax.random.split(jax.random.key(seed), 10)
    facts = centred(streams_of[0], (NF, D), 1.0, 6.0, ((0, 32),))
    dims = centred(streams_of[1], (ND, D), 1.0, 6.0, ((0, 32),))
    tiles = centred(streams_of[2], (LINKS, BLOCK, BLOCK), (5 * LINKS_DEV * BLOCK * BLOCK // (8 * FACT_DEV)) ** -0.5, 0.125, ((0, 32),))
    links = draw_links(jax.random.fold_in(streams_of[9], 71), 0)
    link_count = draw_link_count(jax.random.fold_in(streams_of[9], 71), 0)
    block_table = place_ends(jax.random.randint(streams_of[5], (DBLOCKS,), 0, TABLES), jax.random.fold_in(streams_of[5], 1), 0, TABLES - 1).astype(jnp.int32)
    w_self = centred(streams_of[6], (D, D), D ** -0.5, 0.25)
    w_tables = centred(streams_of[7], (TABLES, D, D), D ** -0.5, 0.25)
    cot = centred(streams_of[8], (NF, D), 1.0, 6.0, ((0, 32),))
    return dict(facts=facts, dims=dims, tiles=tiles, links=links, link_count=link_count, block_table=block_table, w_self=w_self, w_tables=w_tables, cot=cot)


def project_rows(rows, row_table, w_tables):
    acc = jnp.zeros((rows.shape[0], w_tables.shape[2]), jnp.float32)
    for table in range(TABLES):
        term = jnp.dot(rows, w_tables[table], preferred_element_type=jnp.float32)
        acc = acc + jnp.where(row_table[:, None] == table, term, jnp.float32(0.0))
    return acc


def reference(facts, dims, tiles, links, link_count, block_table, w_self, w_tables, cot):
    devices = N_FACT * N_DIM
    row_table = jnp.repeat(block_table, BLOCK)
    projected = project_rows(dims, row_table, w_tables).astype(jnp.bfloat16)
    slot = jnp.arange(LINKS, dtype=jnp.int32) % LINKS_DEV
    owner = jnp.arange(LINKS, dtype=jnp.int32) // LINKS_DEV
    live = (slot < link_count[owner]).astype(jnp.float32).reshape(devices, LINKS_DEV)
    tile_dev = tiles.reshape(devices, LINKS_DEV, BLOCK, BLOCK)
    link_dev = links.reshape(devices, LINKS_DEV, 2)
    proj_blocks = projected.reshape(ND // BLOCK, BLOCK, D)

    def forward_step(acc, xs):
        tile, link, alive = xs
        blocks = proj_blocks[link[:, 1]].astype(jnp.float32)
        contrib = jnp.einsum('lij,ljd->lid', tile.astype(jnp.float32), blocks) * alive[:, None, None]
        return acc.at[link[:, 0]].add(contrib), None

    agg, _ = lax.scan(forward_step, jnp.zeros((NF // BLOCK, BLOCK, D), jnp.float32), (tile_dev, link_dev, live))
    pre = jnp.dot(facts, w_self, preferred_element_type=jnp.float32) + agg.reshape(NF, D)
    fact_out = jax.nn.silu(pre).astype(jnp.bfloat16)
    sig = jax.nn.sigmoid(pre)
    grad_pre = (cot.astype(jnp.float32) * sig * (1.0 + pre * (1.0 - sig))).astype(jnp.bfloat16)
    grad_w_self = lax.dot_general(facts, grad_pre, (((0,), (0,)), ((), ())), preferred_element_type=jnp.float32) * (NF ** -0.5)
    grad_blocks = grad_pre.reshape(NF // BLOCK, BLOCK, D)

    def backward_step(acc, xs):
        tile, link, alive = xs
        blocks = grad_blocks[link[:, 0]].astype(jnp.float32)
        contrib = jnp.einsum('lji,ljd->lid', tile.astype(jnp.float32), blocks) * alive[:, None, None]
        return acc.at[link[:, 1]].add(contrib), None

    gsum, _ = lax.scan(backward_step, jnp.zeros((ND // BLOCK, BLOCK, D), jnp.float32), (tile_dev, link_dev, live))
    gsum_b = gsum.reshape(ND, D).astype(jnp.bfloat16)
    grad_dims = jnp.zeros((ND, D), jnp.float32)
    grads = []
    for table in range(TABLES):
        term = lax.dot_general(gsum_b, w_tables[table], (((1,), (1,)), ((), ())), preferred_element_type=jnp.float32)
        grad_dims = grad_dims + jnp.where(row_table[:, None] == table, term, jnp.float32(0.0))
        masked = jnp.where(row_table[:, None] == table, dims, jnp.zeros_like(dims))
        grads.append(lax.dot_general(masked, gsum_b, (((0,), (0,)), ((), ())), preferred_element_type=jnp.float32) * (ND ** -0.5))
    grad_w_tables = jnp.stack(grads)
    return (fact_out, grad_dims, grad_w_self, grad_w_tables)
```

```python
import functools

import jax
import jax.numpy as jnp
from jax import lax
from jax.experimental import pallas as pl
from jax.experimental.pallas import tpu as pltpu
from jax.sharding import PartitionSpec as P

MESH = pl.DeviceIdType.MESH
BF = jnp.bfloat16
F32 = jnp.float32
CORES = 2


def dot(a, b):
    return jnp.dot(a, b, preferred_element_type=F32)


def flip(x):
    return x.astype(F32).T.astype(BF)


def prep_kernel(dims_n, links, count, table, tiles, facts, dims, w_tables, adj, proj, chunks, acc):
    n_fact, n_dim = dims_n
    chips = n_dim // CORES
    block = tiles.shape[1]
    f = lax.axis_index("fact")
    d = lax.axis_index("dim")
    acc[...] = jnp.zeros_like(acc)
    own = table[f * n_dim + d]
    proj[...] = dot(dims[...], w_tables[own]).astype(BF)

    def add(l, _):
        i = links[l, 0] - f * n_dim
        row = lax.rem(i, CORES) * chips + lax.div(i, CORES)
        col = lax.div(links[l, 1], n_dim)
        acc[row, col] += tiles[l].astype(F32)
        return 0

    lax.fori_loop(0, count[0], add, 0)
    depth = chunks.shape[1] // 2
    facts_t = flip(facts[...])
    dims_t = flip(dims[...])
    for c in range(chips):
        chunks[c, :depth] = facts_t[c * depth : (c + 1) * depth]
        chunks[c, depth:] = dims_t[c * depth : (c + 1) * depth]
    for i in range(n_dim):
        for j in range(n_fact):
            adj[i * block : (i + 1) * block, j * block : (j + 1) * block] = acc[i, j].astype(BF)


def main_kernel(
    dims_n, table, adj, proj, chunks, facts, cot, w_self, w_tables,
    fact_out, grad_dims, weights,
    panel, adj_t, chunk_all, masked, pre, send1, recv1, mine, send2, recv2, gp, grad,
    send3, recv3, gs, gs_all, w_own, w_send, w_recv,
    a_s, a_r, f_s, f_r, b1_s, b1_r, b2_s, b2_r, c_s, c_r, cp_s, cp_r,
    d_s, d_r, e_s, e_r, w_s, w_r, z_s, z_r, p_s, p_r, q_s, q_r,
):
    n_fact, n_dim = dims_n
    chips = n_dim // CORES
    rows, width = facts.shape
    half = width // CORES
    depth = chunks.shape[1] // 2
    tables = w_tables.shape[0]
    per = n_fact // (tables + 1)
    part = depth // per
    f = lax.axis_index("fact")
    d = lax.axis_index("dim")
    c = lax.div(d, CORES)
    k = lax.rem(d, CORES)
    o = 1 - k
    mate = c * CORES + o
    scale_f = float(rows * n_fact * n_dim) ** -0.5
    started = []

    def send(src, dst, ss, rs, df, dd):
        copy = pltpu.make_async_remote_copy(
            src_ref=src, dst_ref=dst, send_sem=ss, recv_sem=rs,
            device_id=(df, dd), device_id_type=MESH,
        )
        copy.start()
        started.append(copy)
        return copy

    def blk(i):
        return pl.ds(pl.multiple_of(i * rows, rows), rows)

    def up(base, j, n):
        return lax.rem(base + j, n)

    barrier = pltpu.get_barrier_semaphore()
    for j in range(1, n_dim):
        pl.semaphore_signal(barrier, inc=1, device_id=(f, up(d, j, n_dim)), device_id_type=MESH)
    for j in range(1, n_fact):
        pl.semaphore_signal(barrier, inc=1, device_id=(up(f, j, n_fact), d), device_id_type=MESH)
    pl.semaphore_wait(barrier, n_dim + n_fact - 2)

    far = sorted(range(1, n_fact), key=lambda j: abs(2 * j - n_fact))
    copies_a = {
        j: send(proj, panel.at[blk(f)], a_s.at[j], a_r.at[j], up(f, j, n_fact), d) for j in far
    }
    rb = k * chips + c
    copies_f = {}
    for j in range(1, n_dim):
        to = up(d, j, n_dim)
        copies_f[j] = send(
            chunks.at[lax.div(to, CORES)], chunk_all.at[:, blk(rb)], f_s.at[j], f_r.at[j], f, to
        )
    panel[blk(f), :] = proj[...]
    chunk_all[:, blk(rb)] = chunks[c]
    pre[...] = dot(facts[...], w_self[...])
    for i in range(n_dim):
        adj_t[:, i * rows : (i + 1) * rows] = flip(adj[i * rows : (i + 1) * rows, :])
    for j in copies_a:
        copies_a[j].wait_recv()

    group = chips * rows

    def grp(i):
        return pl.ds(pl.multiple_of(i * group, group), group)

    send1[...] = dot(adj[grp(o), :], panel[...]).astype(BF)
    order = list(range(1, chips)) + [0]
    copies_1 = {}
    for j in order:
        at = blk(up(c, j, chips))
        copies_1[j] = send(send1.at[at], recv1.at[at], b1_s.at[j], b1_r.at[j], f, mate)
    mine[...] = dot(adj[grp(k), :], panel[...])
    copies_2 = {}
    for j in order:
        copies_1[j].wait_recv()
        chip = up(c, j, chips)
        total = mine[blk(chip), :] + recv1[blk(chip), :].astype(F32)
        if j:
            send2[j] = total.astype(BF)
            copies_2[j] = send(
                send2.at[j], recv2.at[j], b2_s.at[j], b2_r.at[j], f, chip * CORES + k
            )
        else:
            pre[...] += total
    for j in range(n_dim - 1, 0, -1):
        copies_f[j].wait_recv()
    for i in range(n_dim):
        source = lax.rem(i, chips) * CORES + i // chips
        name = table[f * n_dim + source]
        lanes = slice(i * rows, (i + 1) * rows)
        values = chunk_all[depth:, lanes].astype(F32)
        for t in range(tables):
            masked[t * depth : (t + 1) * depth, lanes] = (
                values * (name == t).astype(F32)
            ).astype(BF)
    total = pre[...]
    for j in range(1, chips):
        copies_2[j].wait_recv()
        total = total + recv2[j].astype(F32)
    sig = 1.0 / (1.0 + jnp.exp(-total))
    fact_out[...] = (total * sig).astype(BF)
    gp[blk(rb), :] = (cot[...].astype(F32) * sig * (1.0 + total * (1.0 - sig))).astype(BF)

    copies_c = {}
    for j in range(1, chips):
        copies_c[j] = send(
            gp.at[blk(rb)], gp.at[blk(rb)], c_s.at[j], c_r.at[j], f, up(c, j, chips) * CORES + k
        )
    copies_m = [send(gp.at[blk(rb)], gp.at[blk(rb)], cp_s.at[0], cp_r.at[0], f, mate)]
    for j in range(1, chips):
        copies_c[j].wait_recv()
        at = blk(k * chips + up(c, chips - j, chips))
        copies_m.append(send(gp.at[at], gp.at[at], cp_s.at[j], cp_r.at[j], f, mate))
    grad[...] = dot(adj_t[:, grp(k)], gp[grp(k), :])
    for copy in copies_m:
        copy.wait_recv()
    grad[...] += dot(adj_t[:, grp(o)], gp[grp(o), :])
    copies_d = {}
    for j in far:
        to = up(f, j, n_fact)
        send3[j] = grad[blk(to), :].astype(BF)
        copies_d[j] = send(send3.at[j], recv3.at[j], d_s.at[j], d_r.at[j], to, d)
    side = pl.ds(pl.multiple_of(k * half, half), half)
    w_own[:depth, :] = dot(chunk_all[:depth, :], gp[:, side]) * scale_f
    total = grad[blk(f), :]
    for j in far:
        copies_d[j].wait_recv()
        total = total + recv3[j].astype(F32)
    rounded = total.astype(BF)
    for h in range(CORES):
        gs[h] = rounded[:, h * half : (h + 1) * half]
    copies_e = []
    for j in range(1, n_dim):
        to = up(d, j, n_dim)
        copies_e.append(
            send(gs.at[lax.rem(to, CORES)], gs_all.at[blk(rb)], e_s.at[j], e_r.at[j], f, to)
        )
    gs_all[blk(rb), :] = gs[k]
    own = table[f * n_dim + d]
    grad_dims[...] = lax.dot_general(
        rounded, w_tables[own], (((1,), (1,)), ((), ())), preferred_element_type=F32
    )
    for copy in copies_e:
        copy.wait_recv()
    w_own[depth:, :] = dot(masked[...], gs_all[...]) * scale_f

    def unit(i):
        return pl.ds(pl.multiple_of(i * part, part), part)

    copies_w = {}
    for j in far:
        to = up(f, j, n_fact)
        w_send[j] = w_own[unit(to), :].astype(BF)
        copies_w[j] = send(w_send.at[j], w_recv.at[j], w_s.at[j], w_r.at[j], to, d)
    total = w_own[unit(f), :]
    for j in far:
        copies_w[j].wait_recv()
        total = total + w_recv[j].astype(F32)

    def place(ff, cc, kk):
        return (
            lax.div(ff, per),
            pl.ds(pl.multiple_of(cc * depth + lax.rem(ff, per) * part, part), part),
            pl.ds(pl.multiple_of(kk * half, half), half),
        )

    home = place(f, c, k)
    weights[home] = total.astype(BF)

    def region(ff, cc, kk):
        return weights.at[place(ff, cc, kk)]

    copies_z, copies_p, copies_q = {}, {}, []

    def spread(i):
        src = region(up(f, n_fact - i, n_fact), c, k)
        for j in range(1, chips):
            copies_p[i, j] = send(
                src, src, p_s.at[i, j], p_r.at[i, j], f, up(c, j, chips) * CORES + k
            )
        copies_q.append(send(src, src, q_s.at[i, 0], q_r.at[i, 0], f, mate))

    for j in far:
        copies_z[j] = send(
            region(f, c, k), region(f, c, k), z_s.at[j], z_r.at[j], up(f, j, n_fact), d
        )
    spread(0)
    near = sorted(range(1, n_fact), key=lambda j: min(j, n_fact - j))
    for i in near:
        copies_z[i].wait_recv()
        spread(i)
    for i in [0] + near:
        for j in range(1, chips):
            copies_p[i, j].wait_recv()
            src = region(up(f, n_fact - i, n_fact), up(c, chips - j, chips), k)
            copies_q.append(send(src, src, q_s.at[i, j], q_r.at[i, j], f, mate))
    for copy in copies_q:
        copy.wait_recv()
    for copy in started:
        copy.wait_send()


def body(facts, dims, tiles, links, link_count, block_table, w_self, w_tables, cot):
    n_fact = lax.axis_size("fact")
    n_dim = lax.axis_size("dim")
    chips = n_dim // CORES
    rows, width = facts.shape
    block = tiles.shape[1]
    tables = w_tables.shape[0]
    depth = width // chips
    half = width // CORES
    part = depth * (tables + 1) // n_fact
    dims_n = (n_fact, n_dim)
    vmem = pl.BlockSpec(memory_space=pltpu.VMEM)
    smem = pl.BlockSpec(memory_space=pltpu.SMEM)
    adj, proj, chunks = pl.pallas_call(
        functools.partial(prep_kernel, dims_n),
        out_shape=(
            jax.ShapeDtypeStruct((n_dim * rows, n_fact * rows), BF),
            jax.ShapeDtypeStruct((rows, width), BF),
            jax.ShapeDtypeStruct((chips, 2 * depth, rows), BF),
        ),
        in_specs=[smem, smem, smem, vmem, vmem, vmem, vmem],
        out_specs=(vmem, vmem, vmem),
        scratch_shapes=[pltpu.VMEM((n_dim, n_fact, block, block), F32)],
    )(links, link_count, block_table, tiles, facts, dims, w_tables)
    dma = pltpu.SemaphoreType.DMA
    fact_out, grad_dims, weights = pl.pallas_call(
        functools.partial(main_kernel, dims_n),
        out_shape=(
            jax.ShapeDtypeStruct((rows, width), BF),
            jax.ShapeDtypeStruct((rows, width), F32),
            jax.ShapeDtypeStruct((tables + 1, width, width), BF),
        ),
        in_specs=[smem] + [vmem] * 7,
        out_specs=(vmem, vmem, vmem),
        scratch_shapes=[
            pltpu.VMEM((n_fact * rows, width), BF),
            pltpu.VMEM((n_fact * rows, n_dim * rows), BF),
            pltpu.VMEM((2 * depth, n_dim * rows), BF),
            pltpu.VMEM((tables * depth, n_dim * rows), BF),
            pltpu.VMEM((rows, width), F32),
            pltpu.VMEM((chips * rows, width), BF),
            pltpu.VMEM((chips * rows, width), BF),
            pltpu.VMEM((chips * rows, width), F32),
            pltpu.VMEM((chips, rows, width), BF),
            pltpu.VMEM((chips, rows, width), BF),
            pltpu.VMEM((n_dim * rows, width), BF),
            pltpu.VMEM((n_fact * rows, width), F32),
            pltpu.VMEM((n_fact, rows, width), BF),
            pltpu.VMEM((n_fact, rows, width), BF),
            pltpu.VMEM((CORES, rows, half), BF),
            pltpu.VMEM((n_dim * rows, half), BF),
            pltpu.VMEM(((tables + 1) * depth, half), F32),
            pltpu.VMEM((n_fact, part, half), BF),
            pltpu.VMEM((n_fact, part, half), BF),
            dma((n_fact,)), dma((n_fact,)),
            dma((n_dim,)), dma((n_dim,)),
            dma((chips,)), dma((chips,)),
            dma((chips,)), dma((chips,)),
            dma((chips,)), dma((chips,)),
            dma((chips,)), dma((chips,)),
            dma((n_fact,)), dma((n_fact,)),
            dma((n_dim,)), dma((n_dim,)),
            dma((n_fact,)), dma((n_fact,)),
            dma((n_fact,)), dma((n_fact,)),
            dma((n_fact, chips)), dma((n_fact, chips)),
            dma((n_fact, chips)), dma((n_fact, chips)),
        ],
        compiler_params=pltpu.CompilerParams(collective_id=0, has_side_effects=True),
    )(block_table, adj, proj, chunks, facts, cot, w_self, w_tables)
    return fact_out, grad_dims, weights[0].astype(F32), weights[1:].astype(F32)


def solution(mesh):
    rows = P(("fact", "dim"), None)
    placed = (
        rows,
        rows,
        P(("fact", "dim"), None, None),
        rows,
        P(("fact", "dim")),
        P(),
        P(),
        P(),
        rows,
    )
    return jax.shard_map(
        body,
        mesh=mesh,
        in_specs=placed,
        out_specs=(rows, rows, P(), P()),
        check_vma=False,
    )
```

```python
import functools

import jax
import jax.numpy as jnp
from jax import lax
from jax.experimental import pallas as pl
from jax.experimental.pallas import tpu as pltpu
from jax.sharding import PartitionSpec as P

MESH = pl.DeviceIdType.MESH
BF = jnp.bfloat16
F32 = jnp.float32
CORES = 2
STAGES = 2


def dot(a, b):
    return jnp.dot(a, b, preferred_element_type=F32)


def flip(x):
    return x.astype(F32).T.astype(BF)


def prep_kernel(dims_n, links, count, table, tiles, facts, dims, w_tables, adj, proj, chunks, acc):
    n_fact, n_dim = dims_n
    chips = n_dim // CORES
    block = tiles.shape[1]
    f = lax.axis_index("fact")
    d = lax.axis_index("dim")
    acc[...] = jnp.zeros_like(acc)
    own = table[f * n_dim + d]
    both = dot(dims[...], w_tables[own]).astype(BF)
    cut = proj.shape[2]
    for h in range(proj.shape[0]):
        proj[h] = both[:, h * cut : (h + 1) * cut]

    def add(l, _):
        i = links[0, l] - f * n_dim
        row = lax.rem(i, CORES) * chips + lax.div(i, CORES)
        col = lax.div(links[1, l], n_dim)
        acc[row, col] += tiles[l].astype(F32)
        return 0

    lax.fori_loop(0, count[0], add, 0)
    depth = chunks.shape[1] // 2
    facts_t = flip(facts[...])
    dims_t = flip(dims[...])
    for c in range(chips):
        chunks[c, :depth] = facts_t[c * depth : (c + 1) * depth]
        chunks[c, depth:] = dims_t[c * depth : (c + 1) * depth]
    for i in range(n_dim):
        for j in range(n_fact):
            adj[i * block : (i + 1) * block, j * block : (j + 1) * block] = acc[i, j].astype(BF)


def main_kernel(
    dims_n, table, adj, proj, chunks, facts, cot, w_self, w_tables,
    fact_out, grad_dims, weights,
    panel, adj_t, chunk_all, masked, pre, send1, recv1, mine, send2, recv2, gp, grad,
    send3, recv3, gs, gs_all, w_own, w_send, w_recv,
    a_s, a_r, f_s, f_r, b1_s, b1_r, b2_s, b2_r, c_s, c_r, cp_s, cp_r,
    d_s, d_r, e_s, e_r, w_s, w_r, z_s, z_r, p_s, p_r, q_s, q_r,
):
    n_fact, n_dim = dims_n
    chips = n_dim // CORES
    rows, width = facts.shape
    cut = width // STAGES
    thin = cut // CORES
    depth = chunks.shape[1] // 2
    tables = w_tables.shape[0]
    per = n_fact // (tables + 1)
    part = depth // per
    f = lax.axis_index("fact")
    d = lax.axis_index("dim")
    c = lax.div(d, CORES)
    k = lax.rem(d, CORES)
    o = 1 - k
    mate = c * CORES + o
    scale_f = float(rows * n_fact * n_dim) ** -0.5
    started = []

    def send(src, dst, ss, rs, df, dd):
        copy = pltpu.make_async_remote_copy(
            src_ref=src, dst_ref=dst, send_sem=ss, recv_sem=rs,
            device_id=(df, dd), device_id_type=MESH,
        )
        copy.start()
        started.append(copy)
        return copy

    def blk(i):
        return pl.ds(pl.multiple_of(i * rows, rows), rows)

    def cols(h):
        return slice(h * cut, (h + 1) * cut)

    def up(base, j, n):
        return lax.rem(base + j, n)

    barrier = pltpu.get_barrier_semaphore()
    for j in range(1, n_dim):
        pl.semaphore_signal(barrier, inc=1, device_id=(f, up(d, j, n_dim)), device_id_type=MESH)
    for j in range(1, n_fact):
        pl.semaphore_signal(barrier, inc=1, device_id=(up(f, j, n_fact), d), device_id_type=MESH)
    pl.semaphore_wait(barrier, n_dim + n_fact - 2)

    far = sorted(range(1, n_fact), key=lambda j: abs(2 * j - n_fact))
    near = sorted(range(1, n_fact), key=lambda j: min(j, n_fact - j))
    every = range(STAGES)
    rb = k * chips + c
    copies_a = {}
    for h in every:
        for j in far:
            copies_a[h, j] = send(
                proj.at[h], panel.at[h, blk(f)], a_s.at[h, j], a_r.at[h, j], up(f, j, n_fact), d
            )
    copies_f = {}
    for j in range(1, n_dim):
        to = up(d, j, n_dim)
        copies_f[j] = send(
            chunks.at[lax.div(to, CORES)], chunk_all.at[:, blk(rb)], f_s.at[j], f_r.at[j], f, to
        )
    for h in every:
        panel[h, blk(f), :] = proj[h]
        pre[h] = dot(facts[...], w_self[:, cols(h)])
    chunk_all[:, blk(rb)] = chunks[c]
    for i in range(n_dim):
        adj_t[:, i * rows : (i + 1) * rows] = flip(adj[i * rows : (i + 1) * rows, :])

    group = chips * rows

    def grp(i):
        return pl.ds(pl.multiple_of(i * group, group), group)

    order = list(range(1, chips)) + [0]
    copies_1, copies_2, copies_c, copies_m = {}, {}, {}, {}

    def forward(h):
        for j in far:
            copies_a[h, j].wait_recv()
        send1[h] = dot(adj[grp(o), :], panel[h]).astype(BF)
        for j in order:
            at = blk(up(c, j, chips))
            copies_1[h, j] = send(
                send1.at[h, at], recv1.at[h, at], b1_s.at[h, j], b1_r.at[h, j], f, mate
            )
        mine[h] = dot(adj[grp(k), :], panel[h])

    def pair(h):
        for j in order:
            copies_1[h, j].wait_recv()
            chip = up(c, j, chips)
            total = mine[h, blk(chip), :] + recv1[h, blk(chip), :].astype(F32)
            if j:
                send2[h, j] = total.astype(BF)
                copies_2[h, j] = send(
                    send2.at[h, j], recv2.at[h, j], b2_s.at[h, j], b2_r.at[h, j],
                    f, chip * CORES + k,
                )
            else:
                pre[h] += total

    def activate(h):
        total = pre[h]
        for j in range(1, chips):
            copies_2[h, j].wait_recv()
            total = total + recv2[h, j].astype(F32)
        sig = 1.0 / (1.0 + jnp.exp(-total))
        gp[h, blk(rb), :] = (
            cot[:, cols(h)].astype(F32) * sig * (1.0 + total * (1.0 - sig))
        ).astype(BF)
        src = gp.at[h, blk(rb)]
        for j in range(1, chips):
            copies_c[h, j] = send(
                src, src, c_s.at[h, j], c_r.at[h, j], f, up(c, j, chips) * CORES + k
            )
        copies_m[h, 0] = send(src, src, cp_s.at[h, 0], cp_r.at[h, 0], f, mate)
        fact_out[:, cols(h)] = (total * sig).astype(BF)

    def share(h):
        for j in range(1, chips):
            copies_c[h, j].wait_recv()
            src = gp.at[h, blk(k * chips + up(c, chips - j, chips))]
            copies_m[h, j] = send(src, src, cp_s.at[h, j], cp_r.at[h, j], f, mate)

    def mask():
        for j in range(1, n_dim):
            copies_f[j].wait_recv()
        for i in range(n_dim):
            source = (i % chips) * CORES + i // chips
            name = table[f * n_dim + source]
            lanes = slice(i * rows, (i + 1) * rows)
            values = chunk_all[depth:, lanes].astype(F32)
            for t in range(tables):
                masked[t * depth : (t + 1) * depth, lanes] = (
                    values * (name == t).astype(F32)
                ).astype(BF)

    copies_d, copies_e, copies_w = {}, {}, {}

    def backward(h):
        grad[h] = dot(adj_t[:, grp(k)], gp[h, grp(k), :])
        for j in range(chips):
            copies_m[h, j].wait_recv()
        grad[h] += dot(adj_t[:, grp(o)], gp[h, grp(o), :])
        for j in far:
            to = up(f, j, n_fact)
            send3[h, j] = grad[h, blk(to), :].astype(BF)
            copies_d[h, j] = send(
                send3.at[h, j], recv3.at[h, j], d_s.at[h, j], d_r.at[h, j], to, d
            )

    side = pl.ds(pl.multiple_of(k * thin, thin), thin)

    def own_weight(h):
        w_own[h, :depth, :] = dot(chunk_all[:depth, :], gp[h, :, side]) * scale_f

    def collect(h):
        total = grad[h, blk(f), :]
        for j in near:
            copies_d[h, j].wait_recv()
            total = total + recv3[h, j].astype(F32)
        rounded = total.astype(BF)
        for i in range(CORES):
            gs[h, i] = rounded[:, i * thin : (i + 1) * thin]
        for j in range(1, n_dim):
            to = up(d, j, n_dim)
            copies_e[h, j] = send(
                gs.at[h, lax.rem(to, CORES)], gs_all.at[h, blk(rb)], e_s.at[h, j], e_r.at[h, j],
                f, to,
            )
        gs_all[h, blk(rb), :] = gs[h, k]
        own = table[f * n_dim + d]
        term = lax.dot_general(
            rounded, w_tables[own, :, cols(h)], (((1,), (1,)), ((), ())),
            preferred_element_type=F32,
        )
        if h:
            grad_dims[...] += term
        else:
            grad_dims[...] = term

    def unit(i):
        return pl.ds(pl.multiple_of(i * part, part), part)

    def table_weight(h):
        for j in range(1, n_dim):
            copies_e[h, j].wait_recv()
        w_own[h, depth:, :] = dot(masked[...], gs_all[h]) * scale_f
        for j in far:
            to = up(f, j, n_fact)
            w_send[h, j] = w_own[h, unit(to), :].astype(BF)
            copies_w[h, j] = send(
                w_send.at[h, j], w_recv.at[h, j], w_s.at[h, j], w_r.at[h, j], to, d
            )

    def place(h, ff, cc, kk):
        return (
            lax.div(ff, per),
            pl.ds(pl.multiple_of(cc * depth + lax.rem(ff, per) * part, part), part),
            pl.ds(pl.multiple_of(h * cut + kk * thin, thin), thin),
        )

    def region(h, ff, cc, kk):
        return weights.at[place(h, ff, cc, kk)]

    copies_z, copies_p, copies_q = {}, {}, []

    def spread(h, i):
        src = region(h, up(f, n_fact - i, n_fact), c, k)
        for j in range(1, chips):
            copies_p[h, i, j] = send(
                src, src, p_s.at[h, i, j], p_r.at[h, i, j], f, up(c, j, chips) * CORES + k
            )
        copies_q.append(send(src, src, q_s.at[h, i, 0], q_r.at[h, i, 0], f, mate))

    def finish(h):
        total = w_own[h, unit(f), :]
        for j in near:
            copies_w[h, j].wait_recv()
            total = total + w_recv[h, j].astype(F32)
        weights[place(h, f, c, k)] = total.astype(BF)
        src = region(h, f, c, k)
        for j in far:
            copies_z[h, j] = send(
                src, src, z_s.at[h, j], z_r.at[h, j], up(f, j, n_fact), d
            )
        spread(h, 0)

    def relay(h):
        for i in near:
            copies_z[h, i].wait_recv()
            spread(h, i)

    def hand(h):
        for i in [0] + near:
            for j in range(1, chips):
                copies_p[h, i, j].wait_recv()
                src = region(h, up(f, n_fact - i, n_fact), up(c, chips - j, chips), k)
                copies_q.append(send(src, src, q_s.at[h, i, j], q_r.at[h, i, j], f, mate))

    forward(0)
    pair(0)
    forward(1)
    activate(0)
    pair(1)
    mask()
    share(0)
    activate(1)
    backward(0)
    own_weight(0)
    share(1)
    backward(1)
    own_weight(1)
    collect(0)
    table_weight(0)
    collect(1)
    finish(0)
    table_weight(1)
    relay(0)
    finish(1)
    hand(0)
    relay(1)
    hand(1)
    for copy in copies_q:
        copy.wait_recv()
    for copy in started:
        copy.wait_send()


def post_kernel(cuts, out_in, dims_in, weights, fact_out, grad_dims, w_self, w_tables):
    step = pl.program_id(0)

    @pl.when(step == 0)
    def _():
        fact_out[...] = out_in[...]
        grad_dims[...] = dims_in[...]

    @pl.when(step < cuts)
    def _():
        w_self[...] = weights[0].astype(F32)

    @pl.when(step >= cuts)
    def _():
        w_tables[...] = weights[...].astype(F32)


def body(facts, dims, tiles, links, link_count, block_table, w_self, w_tables, cot):
    n_fact = lax.axis_size("fact")
    n_dim = lax.axis_size("dim")
    chips = n_dim // CORES
    rows, width = facts.shape
    block = tiles.shape[1]
    tables = w_tables.shape[0]
    depth = width // chips
    cut = width // STAGES
    thin = cut // CORES
    part = depth * (tables + 1) // n_fact
    dims_n = (n_fact, n_dim)
    vmem = pl.BlockSpec(memory_space=pltpu.VMEM)
    smem = pl.BlockSpec(memory_space=pltpu.SMEM)
    adj, proj, chunks = pl.pallas_call(
        functools.partial(prep_kernel, dims_n),
        out_shape=(
            jax.ShapeDtypeStruct((n_dim * rows, n_fact * rows), BF),
            jax.ShapeDtypeStruct((STAGES, rows, cut), BF),
            jax.ShapeDtypeStruct((chips, 2 * depth, rows), BF),
        ),
        in_specs=[smem, smem, smem, vmem, vmem, vmem, vmem],
        out_specs=(vmem, vmem, vmem),
        scratch_shapes=[pltpu.VMEM((n_dim, n_fact, block, block), F32)],
        name="prep",
    )(links.T, link_count, block_table, tiles, facts, dims, w_tables)

    def sems(*shape):
        return [pltpu.SemaphoreType.DMA((STAGES, *shape))] * 2

    fact_out, grad_dims, weights = pl.pallas_call(
        functools.partial(main_kernel, dims_n),
        out_shape=(
            jax.ShapeDtypeStruct((rows, width), BF),
            jax.ShapeDtypeStruct((rows, width), F32),
            jax.ShapeDtypeStruct((tables + 1, width, width), BF),
        ),
        in_specs=[smem] + [vmem] * 7,
        out_specs=(vmem, vmem, vmem),
        scratch_shapes=[
            pltpu.VMEM((STAGES, n_fact * rows, cut), BF),
            pltpu.VMEM((n_fact * rows, n_dim * rows), BF),
            pltpu.VMEM((2 * depth, n_dim * rows), BF),
            pltpu.VMEM((tables * depth, n_dim * rows), BF),
            pltpu.VMEM((STAGES, rows, cut), F32),
            pltpu.VMEM((STAGES, chips * rows, cut), BF),
            pltpu.VMEM((STAGES, chips * rows, cut), BF),
            pltpu.VMEM((STAGES, chips * rows, cut), F32),
            pltpu.VMEM((STAGES, chips, rows, cut), BF),
            pltpu.VMEM((STAGES, chips, rows, cut), BF),
            pltpu.VMEM((STAGES, n_dim * rows, cut), BF),
            pltpu.VMEM((STAGES, n_fact * rows, cut), F32),
            pltpu.VMEM((STAGES, n_fact, rows, cut), BF),
            pltpu.VMEM((STAGES, n_fact, rows, cut), BF),
            pltpu.VMEM((STAGES, CORES, rows, thin), BF),
            pltpu.VMEM((STAGES, n_dim * rows, thin), BF),
            pltpu.VMEM((STAGES, (tables + 1) * depth, thin), F32),
            pltpu.VMEM((STAGES, n_fact, part, thin), BF),
            pltpu.VMEM((STAGES, n_fact, part, thin), BF),
            *sems(n_fact),
            *[pltpu.SemaphoreType.DMA((n_dim,))] * 2,
            *sems(chips), *sems(chips), *sems(chips), *sems(chips),
            *sems(n_fact), *sems(n_dim), *sems(n_fact), *sems(n_fact),
            *sems(n_fact, chips), *sems(n_fact, chips),
        ],
        compiler_params=pltpu.CompilerParams(collective_id=0, has_side_effects=True),
        name="main",
    )(block_table, adj, proj, chunks, facts, cot, w_self, w_tables)
    cuts = CORES
    tall = width // cuts
    whole = pl.BlockSpec((rows, width), lambda i: (0, 0))
    return pl.pallas_call(
        functools.partial(post_kernel, cuts),
        out_shape=(
            jax.ShapeDtypeStruct((rows, width), BF),
            jax.ShapeDtypeStruct((rows, width), F32),
            jax.ShapeDtypeStruct((width, width), F32),
            jax.ShapeDtypeStruct((tables, width, width), F32),
        ),
        grid=((tables + 1) * cuts,),
        in_specs=[
            whole, whole, pl.BlockSpec((1, tall, width), lambda i: (i // cuts, i % cuts, 0))
        ],
        out_specs=(
            whole,
            whole,
            pl.BlockSpec((tall, width), lambda i: (jnp.minimum(i, cuts - 1), 0)),
            pl.BlockSpec(
                (1, tall, width),
                lambda i: (jnp.maximum(i // cuts - 1, 0), jnp.where(i < cuts, 0, i % cuts), 0),
            ),
        ),
        name="post",
    )(fact_out, grad_dims, weights)


def solution(mesh):
    rows = P(("fact", "dim"), None)
    placed = (
        rows,
        rows,
        P(("fact", "dim"), None, None),
        rows,
        P(("fact", "dim")),
        P(),
        P(),
        P(),
        rows,
    )
    return jax.shard_map(
        body,
        mesh=mesh,
        in_specs=placed,
        out_specs=(rows, rows, P(), P()),
        check_vma=False,
    )
```

```python
import functools

import jax
import jax.numpy as jnp
from jax import lax
from jax.experimental import pallas as pl
from jax.experimental.pallas import tpu as pltpu
from jax.sharding import PartitionSpec as P

MESH = pl.DeviceIdType.MESH
BF = jnp.bfloat16
F32 = jnp.float32
CORES = 2
STAGES = 2


def dot(a, b):
    return jnp.dot(a, b, preferred_element_type=F32)


def flip(x):
    return x.astype(F32).T.astype(BF)


def prep_kernel(dims_n, links, count, table, tiles, facts, dims, w_tables, adj, proj, chunks, acc):
    n_fact, n_dim = dims_n
    chips = n_dim // CORES
    block = tiles.shape[1]
    f = lax.axis_index("fact")
    d = lax.axis_index("dim")
    acc[...] = jnp.zeros_like(acc)
    own = table[f * n_dim + d]
    both = dot(dims[...], w_tables[own]).astype(BF)
    cut = proj.shape[2]
    for h in range(proj.shape[0]):
        proj[h] = both[:, h * cut : (h + 1) * cut]

    def add(l, _):
        i = links[0, l] - f * n_dim
        row = lax.rem(i, CORES) * chips + lax.div(i, CORES)
        col = lax.div(links[1, l], n_dim)
        acc[row, col] += tiles[l].astype(F32)
        return 0

    lax.fori_loop(0, count[0], add, 0)
    depth = chunks.shape[1] // 2
    facts_t = flip(facts[...])
    dims_t = flip(dims[...])
    for c in range(chips):
        chunks[c, :depth] = facts_t[c * depth : (c + 1) * depth]
        chunks[c, depth:] = dims_t[c * depth : (c + 1) * depth]
    for i in range(n_dim):
        for j in range(n_fact):
            adj[i * block : (i + 1) * block, j * block : (j + 1) * block] = acc[i, j].astype(BF)


def main_kernel(
    dims_n, table, adj, proj, chunks, facts, cot, w_self, w_tables,
    fact_out, grad_dims, weights,
    panel, adj_t, chunk_all, masked, pre, send1, recv1, mine, send2, recv2, gp, grad,
    send3, recv3, gs, gs_all, w_own, w_send, w_recv,
    a_s, a_r, f_s, f_r, b1_s, b1_r, b2_s, b2_r, c_s, c_r, cp_s, cp_r,
    d_s, d_r, e_s, e_r, w_s, w_r, z_s, z_r, p_s, p_r, q_s, q_r,
):
    n_fact, n_dim = dims_n
    chips = n_dim // CORES
    rows, width = facts.shape
    cut = width // STAGES
    thin = cut // CORES
    depth = chunks.shape[1] // 2
    tables = w_tables.shape[0]
    per = n_fact // (tables + 1)
    part = depth // per
    f = lax.axis_index("fact")
    d = lax.axis_index("dim")
    c = lax.div(d, CORES)
    k = lax.rem(d, CORES)
    o = 1 - k
    mate = c * CORES + o
    scale_f = float(rows * n_fact * n_dim) ** -0.5
    started = []

    def send(src, dst, ss, rs, df, dd):
        copy = pltpu.make_async_remote_copy(
            src_ref=src, dst_ref=dst, send_sem=ss, recv_sem=rs,
            device_id=(df, dd), device_id_type=MESH,
        )
        copy.start()
        started.append(copy)
        return copy

    def blk(i):
        return pl.ds(pl.multiple_of(i * rows, rows), rows)

    def cols(h):
        return slice(h * cut, (h + 1) * cut)

    def up(base, j, n):
        return lax.rem(base + j, n)

    barrier = pltpu.get_barrier_semaphore()
    for j in range(1, n_dim):
        pl.semaphore_signal(barrier, inc=1, device_id=(f, up(d, j, n_dim)), device_id_type=MESH)
    for j in range(1, n_fact):
        pl.semaphore_signal(barrier, inc=1, device_id=(up(f, j, n_fact), d), device_id_type=MESH)
    pl.semaphore_wait(barrier, n_dim + n_fact - 2)

    far = sorted(range(1, n_fact), key=lambda j: abs(2 * j - n_fact))
    near = sorted(range(1, n_fact), key=lambda j: min(j, n_fact - j))
    every = range(STAGES)
    rb = k * chips + c
    copies_a = {}
    for h in every:
        for j in far:
            copies_a[h, j] = send(
                proj.at[h], panel.at[h, blk(f)], a_s.at[h, j], a_r.at[h, j], up(f, j, n_fact), d
            )
    copies_f = {}
    for j in range(1, n_dim):
        to = up(d, j, n_dim)
        copies_f[j] = send(
            chunks.at[lax.div(to, CORES)], chunk_all.at[:, blk(rb)], f_s.at[j], f_r.at[j], f, to
        )
    for h in every:
        panel[h, blk(f), :] = proj[h]
        pre[h] = dot(facts[...], w_self[:, cols(h)])
    chunk_all[:, blk(rb)] = chunks[c]
    for i in range(n_dim):
        adj_t[:, i * rows : (i + 1) * rows] = flip(adj[i * rows : (i + 1) * rows, :])

    group = chips * rows

    def grp(i):
        return pl.ds(pl.multiple_of(i * group, group), group)

    order = list(range(1, chips)) + [0]
    copies_1, copies_2, copies_c, copies_m = {}, {}, {}, {}

    def forward(h):
        for j in far:
            copies_a[h, j].wait_recv()
        send1[h] = dot(adj[grp(o), :], panel[h]).astype(BF)
        for j in order:
            at = blk(up(c, j, chips))
            copies_1[h, j] = send(
                send1.at[h, at], recv1.at[h, at], b1_s.at[h, j], b1_r.at[h, j], f, mate
            )
        mine[h] = dot(adj[grp(k), :], panel[h])

    def pair(h):
        for j in order:
            copies_1[h, j].wait_recv()
            chip = up(c, j, chips)
            total = mine[h, blk(chip), :] + recv1[h, blk(chip), :].astype(F32)
            if j:
                send2[h, j] = total.astype(BF)
                copies_2[h, j] = send(
                    send2.at[h, j], recv2.at[h, j], b2_s.at[h, j], b2_r.at[h, j],
                    f, chip * CORES + k,
                )
            else:
                pre[h] += total

    def activate(h):
        total = pre[h]
        for j in range(1, chips):
            copies_2[h, j].wait_recv()
            total = total + recv2[h, j].astype(F32)
        sig = 1.0 / (1.0 + jnp.exp(-total))
        gp[h, blk(rb), :] = (
            cot[:, cols(h)].astype(F32) * sig * (1.0 + total * (1.0 - sig))
        ).astype(BF)
        src = gp.at[h, blk(rb)]
        for j in range(1, chips):
            copies_c[h, j] = send(
                src, src, c_s.at[h, j], c_r.at[h, j], f, up(c, j, chips) * CORES + k
            )
        copies_m[h, 0] = send(src, src, cp_s.at[h, 0], cp_r.at[h, 0], f, mate)
        fact_out[:, cols(h)] = (total * sig).astype(BF)

    def share(h):
        for j in range(1, chips):
            copies_c[h, j].wait_recv()
            src = gp.at[h, blk(k * chips + up(c, chips - j, chips))]
            copies_m[h, j] = send(src, src, cp_s.at[h, j], cp_r.at[h, j], f, mate)

    def mask():
        for j in range(1, n_dim):
            copies_f[j].wait_recv()
        for i in range(n_dim):
            source = (i % chips) * CORES + i // chips
            name = table[f * n_dim + source]
            lanes = slice(i * rows, (i + 1) * rows)
            values = chunk_all[depth:, lanes].astype(F32)
            for t in range(tables):
                masked[t * depth : (t + 1) * depth, lanes] = (
                    values * (name == t).astype(F32)
                ).astype(BF)

    copies_d, copies_e, copies_w = {}, {}, {}

    def backward(h):
        grad[h] = dot(adj_t[:, grp(k)], gp[h, grp(k), :])
        for j in range(chips):
            copies_m[h, j].wait_recv()
        grad[h] += dot(adj_t[:, grp(o)], gp[h, grp(o), :])
        for j in far:
            to = up(f, j, n_fact)
            send3[h, j] = grad[h, blk(to), :].astype(BF)
            copies_d[h, j] = send(
                send3.at[h, j], recv3.at[h, j], d_s.at[h, j], d_r.at[h, j], to, d
            )

    side = pl.ds(pl.multiple_of(k * thin, thin), thin)

    def own_weight(h):
        w_own[h, :depth, :] = dot(chunk_all[:depth, :], gp[h, :, side]) * scale_f

    def collect(h):
        total = grad[h, blk(f), :]
        for j in near:
            copies_d[h, j].wait_recv()
            total = total + recv3[h, j].astype(F32)
        rounded = total.astype(BF)
        for i in range(CORES):
            gs[h, i] = rounded[:, i * thin : (i + 1) * thin]
        for j in range(1, n_dim):
            to = up(d, j, n_dim)
            copies_e[h, j] = send(
                gs.at[h, lax.rem(to, CORES)], gs_all.at[h, blk(rb)], e_s.at[h, j], e_r.at[h, j],
                f, to,
            )
        gs_all[h, blk(rb), :] = gs[h, k]
        own = table[f * n_dim + d]
        term = lax.dot_general(
            rounded, w_tables[own, :, cols(h)], (((1,), (1,)), ((), ())),
            preferred_element_type=F32,
        )
        if h:
            grad_dims[...] += term
        else:
            grad_dims[...] = term

    def unit(i):
        return pl.ds(pl.multiple_of(i * part, part), part)

    def table_weight(h):
        for j in range(1, n_dim):
            copies_e[h, j].wait_recv()
        w_own[h, depth:, :] = dot(masked[...], gs_all[h]) * scale_f
        for j in far:
            to = up(f, j, n_fact)
            w_send[h, j] = w_own[h, unit(to), :].astype(BF)
            copies_w[h, j] = send(
                w_send.at[h, j], w_recv.at[h, j], w_s.at[h, j], w_r.at[h, j], to, d
            )

    def place(h, ff, cc, kk):
        return (
            lax.div(ff, per),
            pl.ds(pl.multiple_of(cc * depth + lax.rem(ff, per) * part, part), part),
            pl.ds(pl.multiple_of(h * cut + kk * thin, thin), thin),
        )

    def region(h, ff, cc, kk):
        return weights.at[place(h, ff, cc, kk)]

    copies_z, copies_p, copies_q = {}, {}, []

    def spread(h, i):
        src = region(h, up(f, n_fact - i, n_fact), c, k)
        for j in range(1, chips):
            copies_p[h, i, j] = send(
                src, src, p_s.at[h, i, j], p_r.at[h, i, j], f, up(c, j, chips) * CORES + k
            )
        copies_q.append(send(src, src, q_s.at[h, i, 0], q_r.at[h, i, 0], f, mate))

    def finish(h):
        total = w_own[h, unit(f), :]
        for j in near:
            copies_w[h, j].wait_recv()
            total = total + w_recv[h, j].astype(F32)
        weights[place(h, f, c, k)] = total.astype(BF)
        src = region(h, f, c, k)
        for j in far:
            copies_z[h, j] = send(
                src, src, z_s.at[h, j], z_r.at[h, j], up(f, j, n_fact), d
            )
        spread(h, 0)

    def relay(h):
        for i in near:
            copies_z[h, i].wait_recv()
            spread(h, i)

    def hand(h):
        for i in [0] + near:
            for j in range(1, chips):
                copies_p[h, i, j].wait_recv()
                src = region(h, up(f, n_fact - i, n_fact), up(c, chips - j, chips), k)
                copies_q.append(send(src, src, q_s.at[h, i, j], q_r.at[h, i, j], f, mate))

    forward(0)
    pair(0)
    forward(1)
    activate(0)
    pair(1)
    mask()
    share(0)
    activate(1)
    backward(0)
    own_weight(0)
    share(1)
    backward(1)
    own_weight(1)
    collect(0)
    table_weight(0)
    collect(1)
    finish(0)
    table_weight(1)
    relay(0)
    finish(1)
    hand(0)
    relay(1)
    hand(1)
    for copy in copies_q:
        copy.wait_recv()
    for copy in started:
        copy.wait_send()


def post_kernel(cuts, out_in, dims_in, weights, fact_out, grad_dims, w_self, w_tables):
    step = pl.program_id(0)

    @pl.when(step == 0)
    def _():
        fact_out[...] = out_in[...]
        grad_dims[...] = dims_in[...]

    @pl.when(step < cuts)
    def _():
        w_self[...] = weights[0].astype(F32)

    @pl.when(step >= cuts)
    def _():
        w_tables[...] = weights[...].astype(F32)


def body(facts, dims, tiles, links, link_count, block_table, w_self, w_tables, cot):
    n_fact = lax.axis_size("fact")
    n_dim = lax.axis_size("dim")
    chips = n_dim // CORES
    rows, width = facts.shape
    block = tiles.shape[1]
    tables = w_tables.shape[0]
    depth = width // chips
    cut = width // STAGES
    thin = cut // CORES
    part = depth * (tables + 1) // n_fact
    dims_n = (n_fact, n_dim)
    cells = n_fact * n_dim * rows * rows
    panes = (n_fact + n_dim) * rows * width
    grant = min(62 << 20, 4 * cells + 16 * panes + 8 * tables * width * width + (6 << 20))
    small = min(62 << 20, 8 * cells + 4 * tables * width * width + (6 << 20))
    vmem = pl.BlockSpec(memory_space=pltpu.VMEM)
    smem = pl.BlockSpec(memory_space=pltpu.SMEM)
    adj, proj, chunks = pl.pallas_call(
        functools.partial(prep_kernel, dims_n),
        out_shape=(
            jax.ShapeDtypeStruct((n_dim * rows, n_fact * rows), BF),
            jax.ShapeDtypeStruct((STAGES, rows, cut), BF),
            jax.ShapeDtypeStruct((chips, 2 * depth, rows), BF),
        ),
        in_specs=[smem, smem, smem, vmem, vmem, vmem, vmem],
        out_specs=(vmem, vmem, vmem),
        scratch_shapes=[pltpu.VMEM((n_dim, n_fact, block, block), F32)],
        compiler_params=pltpu.CompilerParams(vmem_limit_bytes=small),
        name="prep",
    )(links.T, link_count, block_table, tiles, facts, dims, w_tables)

    def sems(*shape):
        return [pltpu.SemaphoreType.DMA((STAGES, *shape))] * 2

    fact_out, grad_dims, weights = pl.pallas_call(
        functools.partial(main_kernel, dims_n),
        out_shape=(
            jax.ShapeDtypeStruct((rows, width), BF),
            jax.ShapeDtypeStruct((rows, width), F32),
            jax.ShapeDtypeStruct((tables + 1, width, width), BF),
        ),
        in_specs=[smem] + [vmem] * 7,
        out_specs=(vmem, vmem, vmem),
        scratch_shapes=[
            pltpu.VMEM((STAGES, n_fact * rows, cut), BF),
            pltpu.VMEM((n_fact * rows, n_dim * rows), BF),
            pltpu.VMEM((2 * depth, n_dim * rows), BF),
            pltpu.VMEM((tables * depth, n_dim * rows), BF),
            pltpu.VMEM((STAGES, rows, cut), F32),
            pltpu.VMEM((STAGES, chips * rows, cut), BF),
            pltpu.VMEM((STAGES, chips * rows, cut), BF),
            pltpu.VMEM((STAGES, chips * rows, cut), F32),
            pltpu.VMEM((STAGES, chips, rows, cut), BF),
            pltpu.VMEM((STAGES, chips, rows, cut), BF),
            pltpu.VMEM((STAGES, n_dim * rows, cut), BF),
            pltpu.VMEM((STAGES, n_fact * rows, cut), F32),
            pltpu.VMEM((STAGES, n_fact, rows, cut), BF),
            pltpu.VMEM((STAGES, n_fact, rows, cut), BF),
            pltpu.VMEM((STAGES, CORES, rows, thin), BF),
            pltpu.VMEM((STAGES, n_dim * rows, thin), BF),
            pltpu.VMEM((STAGES, (tables + 1) * depth, thin), F32),
            pltpu.VMEM((STAGES, n_fact, part, thin), BF),
            pltpu.VMEM((STAGES, n_fact, part, thin), BF),
            *sems(n_fact),
            *[pltpu.SemaphoreType.DMA((n_dim,))] * 2,
            *sems(chips), *sems(chips), *sems(chips), *sems(chips),
            *sems(n_fact), *sems(n_dim), *sems(n_fact), *sems(n_fact),
            *sems(n_fact, chips), *sems(n_fact, chips),
        ],
        compiler_params=pltpu.CompilerParams(
            collective_id=0, has_side_effects=True, vmem_limit_bytes=grant
        ),
        name="main",
    )(block_table, adj, proj, chunks, facts, cot, w_self, w_tables)
    cuts = CORES
    tall = width // cuts
    whole = pl.BlockSpec((rows, width), lambda i: (0, 0))
    return pl.pallas_call(
        functools.partial(post_kernel, cuts),
        out_shape=(
            jax.ShapeDtypeStruct((rows, width), BF),
            jax.ShapeDtypeStruct((rows, width), F32),
            jax.ShapeDtypeStruct((width, width), F32),
            jax.ShapeDtypeStruct((tables, width, width), F32),
        ),
        grid=((tables + 1) * cuts,),
        in_specs=[
            whole, whole, pl.BlockSpec((1, tall, width), lambda i: (i // cuts, i % cuts, 0))
        ],
        out_specs=(
            whole,
            whole,
            pl.BlockSpec((tall, width), lambda i: (jnp.minimum(i, cuts - 1), 0)),
            pl.BlockSpec(
                (1, tall, width),
                lambda i: (jnp.maximum(i // cuts - 1, 0), jnp.where(i < cuts, 0, i % cuts), 0),
            ),
        ),
        compiler_params=pltpu.CompilerParams(vmem_limit_bytes=12 << 20),
        name="post",
    )(fact_out, grad_dims, weights)


def solution(mesh):
    rows = P(("fact", "dim"), None)
    placed = (
        rows,
        rows,
        P(("fact", "dim"), None, None),
        rows,
        P(("fact", "dim")),
        P(),
        P(),
        P(),
        rows,
    )
    return jax.shard_map(
        body,
        mesh=mesh,
        in_specs=placed,
        out_specs=(rows, rows, P(), P()),
        check_vma=False,
    )
```
